32 devices in a mesh: group: 2 (over x), expert: 16 (over z, y, core).
Axes of the slice: x: 2, y: 2, z: 4, core: 2. Of those that a mesh axis runs over, the one named last changes fastest.
Arguments:
- tokens: bfloat16 [4096, 7168], P(('group', 'expert')), parts along dimension 0, may hold values from -6 to 6
- expert_ids: int32 [4096, 2], P(('group', 'expert')), parts along dimension 0, may hold values from 0 to 7, all different within a row; in each aligned block of 128 rows (0 to 127, 128 to 255, ...) at most 64 rows name the same one
- gate_weights: float32 [4096, 2], P(('group', 'expert')), parts along dimension 0, may hold values from 0.05 to 1
- slot_expert: int32 [16], replicated, may hold values from 0 to 7, as said below
- w_gate_up: bfloat16 [16, 7168, 1024], P('expert'), may hold values from -0.0625 to 0.0625
- w_down: bfloat16 [16, 512, 7168], P('expert'), may hold values from -0.1875 to 0.1875
Outputs:
- moe_output: bfloat16 [4096, 7168], P(('group', 'expert')), parts along dimension 0
The draws below stay inside these ranges and needn't reach their ends.
There are 2 independent parts, one for each index of `group`. The reference program is written for one: setup_inputs(seed, part) draws one part's arguments, and reference() takes and returns one part's arrays. A program takes and returns all parts, laid end to end along the dimension named above; an argument that names none is the same for every part. Nothing has to cross between parts.
Inputs may be any that keep to these rules, and one draw needn't show every extreme that they name: `expert_ids`: each token names 2 different experts. In the rows of one device (128 tokens) no expert is named more than 64 times, a bound that some block reaches. `slot_expert`: the first 8 slots hold every expert once, and slot s + 8 holds the same expert as slot s.
All inputs are finite; a program needn't handle non-finite values.
Results may differ from the reference program's by a relative error of at most 0.0065.
Values may be sent and summed in bfloat16 or wider, within the bound.
A program may use at most 128 MiB of HBM per device.

```python
import math
import jax
import jax.numpy as jnp
import numpy as np
from jax import lax

D = 7168
FF = 1024
TOP = 2
TOK_DEV = 128
FSH = 512
EXPERTS = 8
MOST = 64
TOKENS = 2048
N_EXPERT = 16


def draw_slot_expert(key, part):
    order = jax.random.permutation(key, EXPERTS).astype(jnp.int32)
    return jnp.concatenate([order, order])


def block_levels(own_key, dims, cuts, least, high):
    factor_of = 1.0
    for position, parts in cuts:
        heights = jax.random.uniform(jax.random.fold_in(jax.random.fold_in(own_key, 6), position), (parts,), jnp.float32, least / len(cuts), high / len(cuts))
        factor_of = factor_of * jnp.repeat(jnp.exp(heights), dims[position] // parts).reshape((-1,) + (1,) * (len(dims) - 1 - position))
    return factor_of


def deal_out(own_key, own, number, rows, amount, top, most, lean):
    ranking = jax.random.permutation(own_key, amount)
    heavy_load, usual = load_shares(amount, rows * top, most, lean, True), load_shares(amount, rows * top, most, lean, False)
    places = jnp.arange(amount)

    def named(sizes, rotation):
        used = int((sizes > 0).sum())
        fixed = max(1, used // 4)
        passed = fixed + (places - fixed + rotation * (used - fixed)) % max(1, amount - fixed)
        return jnp.zeros((amount,), jnp.int32).at[ranking[jnp.where(places < fixed, places, passed)]].set(jnp.asarray(sizes, jnp.int32))

    sizes = jnp.where(number % 4 == 0, named(heavy_load, number // 4), named(usual, number - number // 4 - 1))
    mixed = jax.random.permutation(jax.random.fold_in(own, 3), amount)
    donor, taker = mixed[0:amount // 2 * 2:2], mixed[1:amount // 2 * 2:2]
    room = jnp.minimum(sizes[donor] - 1, most - sizes[taker]) // 2
    room = jnp.where((donor == ranking[0]) | (taker == ranking[0]) | (sizes[taker] == 0), 0, jnp.maximum(room, 0))
    passed = jax.random.randint(jax.random.fold_in(own, 4), (amount // 2,), 0, 1 << 20) % (room + 1)
    sizes = sizes.at[donor].add(-passed).at[taker].add(passed)
    members = jnp.searchsorted(jnp.cumsum(sizes), jnp.arange(rows * top), side="right").astype(jnp.int32)
    grid = members.reshape(top, rows).T
    grid = grid[jax.random.permutation(jax.random.fold_in(own, 1), rows)]
    rotation = jax.random.randint(jax.random.fold_in(own, 2), (rows, 1), 0, top)
    return jnp.take_along_axis(grid, (jnp.arange(top)[None, :] + rotation) % top, axis=1)


def load_shares(count, total, reach, skew, full):
    loads = [(1 << 20) // math.isqrt(rank ** skew) + 1 for rank in range(1, count + 1)]
    largest = reach if full else min(reach, max(-(-total // count), total * loads[0] // sum(loads)))
    least = 1 if total - largest >= count - 1 else 0
    given, rest = [largest] + [least] * (count - 1), total - largest - least * (count - 1)
    while rest > 0:
        free = [i for i in range(1, count) if given[i] < largest] or [i for i in range(1, count) if given[i] < reach]
        mass, remaining = sum([loads[i] for i in free]), rest
        for i in free:
            more = min(reach - given[i], max(1, remaining * loads[i] // mass), rest)
            given[i] = given[i] + more
            rest = rest - more
    return np.array(given)


def scatter_about(stream_key, extent, scale, most, split=(), kind=jnp.bfloat16):
    drawn = jax.random.normal(stream_key, extent, jnp.float32) * scale
    if len(split) > 0:
        drawn = block_levels(stream_key, extent, split, -0.22, 0.18) * drawn
    return jnp.clip(drawn, min=-most, max=most).astype(kind)


def setup_inputs(seed: int = 0, part: int = 0) -> dict:
    key_list = jax.random.split(jax.random.key(seed), 7)
    own_keys = jax.random.split(jax.random.fold_in(key_list[6], part), 7)
    tokens = scatter_about(own_keys[0], (TOKENS, D), 1.0, 6.0, ((0, 16),))
    expert_ids_keys = jax.random.split(jax.random.fold_in(own_keys[1], 1), TOKENS // TOK_DEV)
    expert_ids_turns = jax.random.permutation(jax.random.fold_in(own_keys[1], 3), TOKENS // TOK_DEV)
    expert_ids = jax.vmap(lambda own, number: deal_out(jax.random.fold_in(own_keys[1], 2), own, number, TOK_DEV, EXPERTS, TOP, MOST, 2))(expert_ids_keys, expert_ids_turns).reshape((TOKENS, TOP))
    gate_weights = jnp.clip(jnp.exp(math.log(1.0) - 2.9957323 * jax.random.uniform(own_keys[2], (TOKENS, TOP), jnp.float32) ** block_levels(own_keys[2], (TOKENS, TOP), ((0, 16),), -0.2, 0.2)), 0.05, 1.0)
    slot_expert = draw_slot_expert(jax.random.fold_in(key_list[6], 71), part)
    w_gate_up = scatter_about(key_list[4], (N_EXPERT, D, FF), D ** -0.5, 0.0625, ((0, 16),))
    w_down = scatter_about(key_list[5], (N_EXPERT, FSH, D), FF ** -0.5, 0.1875, ((0, 16),))
    return dict(tokens=tokens, expert_ids=expert_ids, gate_weights=gate_weights, slot_expert=slot_expert, w_gate_up=w_gate_up, w_down=w_down)


def reference(tokens, expert_ids, gate_weights, slot_expert, w_gate_up, w_down):
    choice_total = TOKENS * TOP
    span = N_EXPERT * MOST
    flat_ids = expert_ids.reshape(-1).astype(jnp.int32)
    order = jnp.argsort(flat_ids, stable=True).astype(jnp.int32)
    member = (flat_ids[:, None] == jnp.arange(EXPERTS, dtype=jnp.int32)[None, :]).astype(jnp.int32)
    counts = jnp.sum(member, axis=0).astype(jnp.int32)
    starts = (jnp.cumsum(counts) - counts).astype(jnp.int32)
    padded_order = jnp.concatenate([order, jnp.zeros((span,), jnp.int32)])

    def slot_half(rows, slot):
        projected = jnp.dot(rows, w_gate_up[slot], preferred_element_type=jnp.float32)
        hidden = (jax.nn.silu(projected[:, :FSH]) * projected[:, FSH:]).astype(jnp.bfloat16)
        return jnp.dot(hidden, w_down[slot], preferred_element_type=jnp.float32).astype(jnp.bfloat16)

    def one_expert(slot):
        expert = slot_expert[slot]
        picked = lax.dynamic_slice_in_dim(padded_order, starts[expert], span)
        valid = jnp.arange(span, dtype=jnp.int32) < counts[expert]
        rows = tokens[picked // TOP]
        lower = slot_half(rows, slot)
        upper = slot_half(rows, slot + EXPERTS)
        summed = (lower.astype(jnp.float32) + upper.astype(jnp.float32)).astype(jnp.bfloat16)
        summed = jnp.where(valid[:, None], summed, jnp.zeros_like(summed))
        target = jnp.where(valid, picked, choice_total).astype(jnp.int32)
        return summed, target

    outputs, targets = lax.map(one_expert, jnp.arange(EXPERTS, dtype=jnp.int32))
    table = jnp.zeros((choice_total + 1, D), jnp.bfloat16)
    table = table.at[targets.reshape(-1)].set(outputs.reshape(-1, D))
    chosen = table[:choice_total].reshape(TOKENS, TOP, D)
    total = jnp.sum(gate_weights[:, :, None] * chosen.astype(jnp.float32), axis=1)
    return total.astype(jnp.bfloat16)
```

```python
import jax
import jax.numpy as jnp
import numpy as np
from jax import lax
from jax.experimental import pallas as pl
from jax.experimental.pallas import tpu as pltpu
from jax.sharding import PartitionSpec as P


def nearest(length):
    order = []
    for z in range(length):
        both = min(z, length - 1 - z)
        rest = [(t // 2 + 1, t % 2 == 0) for t in range(2 * both)]
        order.append(rest + [(t - both + 1, 2 * z > length - 1) for t in range(2 * both, length - 1)])
    return order


def pick(z, arrays, keys):
    out = arrays[keys[0]]
    for key in sorted(set(keys)):
        if key != keys[0]:
            hit = (z == np.array([i for i, k in enumerate(keys) if k == key])).any()
            out = jnp.where(hit, arrays[key], out)
    return out


def add(*terms):
    total = terms[0].astype(jnp.float32)
    for term in terms[1:]:
        total = total + term.astype(jnp.float32)
    return total.astype(jnp.bfloat16)


def per_device(tokens, expert_ids, gate_weights, slot_expert, w_gate_up, w_down):
    devices = lax.axis_size("expert")
    experts = devices // 2
    length = devices // 4
    rows, width = tokens.shape
    half = w_down.shape[1]
    me = lax.axis_index("expert")
    z, y, c = me // 4, me // 2 % 2, me % 2

    def line(x, step, who):
        return lax.ppermute(x, "expert", [(4 * i + j, 4 * (i + step) + j) for i in who for j in range(4)])

    def across(x):
        return lax.ppermute(x, "expert", [(i, i ^ 2) for i in range(devices)])

    def other_core(x):
        return lax.ppermute(x, "expert", [(i, i ^ 1) for i in range(devices)])

    chosen = expert_ids[:, :, None] == slot_expert[None, None, :experts]
    weights = jnp.sum(jnp.where(chosen, gate_weights[:, :, None], 0.0), axis=1)
    all_weights = lax.all_gather(weights, "expert", axis=0, tiled=False)
    mine = lax.dynamic_index_in_dim(all_weights, lax.rem(me, experts), axis=2, keepdims=False)

    order = nearest(length)
    mine, up, down = lax.optimization_barrier((mine, tokens, tokens))
    arrived, sums, chips = {}, {}, {}
    last = length - 2

    def halves(block, home):
        def rows_of(x, a):
            gates = jnp.concatenate([mine[4 * home + 2 * a + b] for b in (c, 1 - c)])
            return jnp.concatenate([x, other_core(x)], axis=0), gates[:, None]
        return rows_of(block, y), rows_of(across(block), 1 - y)

    def expert(parts):
        group = jnp.concatenate([part[0] for part in parts], axis=0)
        w = jnp.concatenate([part[1] for part in parts], axis=0)
        projected = jnp.dot(group, w_gate_up[0], preferred_element_type=jnp.float32)
        hidden = (jax.nn.silu(projected[:, :half]) * projected[:, half:]).astype(jnp.bfloat16)
        partial = (jnp.dot(hidden, w_down[0], preferred_element_type=jnp.float32) * w).astype(jnp.bfloat16)
        out = []
        for i in range(len(parts)):
            own = partial[2 * i * rows:(2 * i + 1) * rows]
            out.append(add(own, other_core(partial[(2 * i + 1) * rows:(2 * i + 2) * rows])))
        return out

    waiting, names = list(halves(tokens, z)), [(-1, 0), (-1, 1)]
    for s in range(1, length):
        up = line(up, 1, range(s - 1, length - 1))
        down = line(down, -1, range(1, length - s + 1))
        arrived[(s, True)], arrived[(s, False)] = up, down
        t = s - 1
        block = pick(z, arrived, [order[i][t] for i in range(length)])
        if t < last:
            block, up, down = lax.optimization_barrier((block, up, down))
        elif (-1, 0) in chips:
            block, chips[(-1, 0)] = lax.optimization_barrier((block, chips[(-1, 0)]))
        home = jnp.asarray([i - order[i][t][0] * (1 if order[i][t][1] else -1) for i in range(length)], jnp.int32)[z]
        near, far = halves(block, home)
        waiting.append(near)
        names.append((t, 0))
        if t < last:
            waiting.append(far)
            names.append((t, 1))
        if t != last - 1:
            chips.update(zip(names, expert(waiting)))
            waiting, names = [], []
    chips.update(zip([(last, 1)], expert([far])))
    index = [{(s, d): t for t, (s, d) in enumerate(order[i])} for i in range(length)]
    rising = {s: [index[i].get((s, False), last) for i in range(length)] for s in range(1, length)}
    falling = {s: [index[i].get((s, True), last) for i in range(length)] for s in range(1, length)}
    got, picked = None, {}

    def settle(t, got):
        sums[t] = add(chips[(t, 0)], got)
        ready = [s for s in rising if s not in picked and set(rising[s] + falling[s]) <= set(sums)]
        for s in reversed(ready):
            picked[s] = lax.optimization_barrier((pick(z, sums, rising[s]), pick(z, sums, falling[s])))
        return ready

    for t in [last - 1, last] + list(range(last - 2, -2, -1)):
        leave = chips[(t, 1)]
        if got is not None:
            leave, got = lax.optimization_barrier((leave, got))
            for s in settle(before, got):
                leave, picked[s] = lax.optimization_barrier((leave, picked[s]))
        got, before = across(leave), t
    settle(before, got)
    from_below = from_above = None
    for s in reversed(range(1, length)):
        rise, fall = picked[s]
        if from_below is not None:
            rise, fall = add(rise, from_below), add(fall, from_above)
        from_below = line(rise, 1, range(0, length - s))
        from_above = line(fall, -1, range(s, length))
    return add(sums[-1], from_below, from_above)


ORDER = (
    (
        "SyA0", "SpA0", "SiA0", "SpC0", "C00", "SiC0", "SyC0", "SpB0", "SpA1", "SyA1", "C10", "SpD0",
        "SiD0", "SpC1", "C01", "C20", "RB0", "SpA2", "SpB1", "C02", "SyA2", "SpD1", "C11", "C21",
        "SpA3", "SyA3", "RC1", "SpB2", "C03", "SpC3", "RD1", "C12", "SpD3", "RB1", "SpB3", "C23",
        "SpC2", "RB2", "C13", "SpD2", "RC3", "RD3", "C22", "RB3", "RA2", "RC2", "RA3", "RD0",
        "RD2", "RC0", "RA1", "RA0",
    ),
    (
        "SpA1", "SoA1", "SiA1", "SyA1", "SpC1", "C01", "SyC1", "SoC1", "SiC1", "SpA2", "SpA0", "SpB1",
        "SoA2", "SiA0", "SyA0", "C02", "SpD1", "SpC0", "SpC2", "C00", "C11", "SyA2", "SiD1", "SoD1",
        "SpD0", "C21", "SpA3", "SoA3", "SpB0", "SiC0", "C20", "SyA3", "SiD0", "SpD2", "C03", "SpB2",
        "SpC3", "SoC3", "C10", "RB1", "SpD3", "SoD3", "C12", "SpB3", "C23", "SoC2", "RB2", "C13",
        "SoD2", "C22", "RB3", "RB0", "RC3", "RD3", "RC0", "RD0", "RA2", "RC2", "RA3", "RD2",
        "RA0", "RA1", "RD1", "RC1",
    ),
)


HEAD, SPAN = 80, 128
PAIR = 96
MESH = pl.DeviceIdType.MESH
PLACE = (0, 1)
UNIT = {"A": 0, "B": 1, "C": 2, "D": 2}
LETTER = "ABCD"


def incoming(role, p, k):
    if p == "B":
        return []
    at = PLACE[role]
    sides = {0: ["i"], 1: ["o"] if role else [], -1: ["i"]}
    if k == at:
        got = ["i", "o"] if role else ["i"]
    elif k > at:
        got = ["o"] if role else []
    else:
        got = ["i"]
    if p == "A" or (p == "C" and k == at):
        got = got + ["y"]
    return got


def outgoing(role, p, k):
    if p == "B":
        return "y"
    at = PLACE[role]
    if k == at:
        return "f" if p in "AC" else "y"
    return "o" if k < at else "i"


def rows_of(p):
    return (0, HEAD) if p in "AB" else (HEAD, SPAN - HEAD)


def held_rows(p):
    return {"A": (0, HEAD), "B": (0, HEAD), "C": (0, SPAN - HEAD), "D": (PAIR // 2, SPAN - HEAD)}[p]


def fused_kernel(tok, w1_any, w2_any, out, x, pp, ry, ryc, rza, rzc, w1, w2, left, hid, held, ps, land,
                 wsem, lsem, isem, osem, xs, xr, ps_send, pr, rs, rry, rrz):
    width = w2.shape[1]
    half = w2.shape[0]
    experts = lax.axis_size("expert") // 2
    me = lax.axis_index("expert")
    z, y, c = me // 4, me // 2 % 2, me % 2
    low = z < 2
    middle = (z == 1) | (z == 2)
    inner = jnp.where(low, z + 1, z - 1)
    outer = jnp.where(low, jnp.maximum(z - 1, 0), jnp.minimum(z + 1, 3))
    where = {
        "i": {"expert": 4 * inner + 2 * y + c},
        "o": {"expert": 4 * outer + 2 * y + c},
        "y": {"expert": 4 * z + 2 * (1 - y) + c},
        "p": {"expert": 4 * z + 2 * y + 1 - c},
    }
    DEST = "ioyp"

    def real(k):
        return jnp.where(low, k, 3 - k)

    weight_copies = [
        pltpu.make_async_copy(w1_any.at[0], w1, wsem.at[0]),
        pltpu.make_async_copy(w2_any.at[0], w2, wsem.at[1]),
    ]
    for copy in weight_copies:
        copy.start()

    barrier = pltpu.get_barrier_semaphore()
    for d in "iyp":
        pl.semaphore_signal(barrier, inc=1, device_id=where[d], device_id_type=MESH)

    @pl.when(middle)
    def _():
        pl.semaphore_signal(barrier, inc=1, device_id=where["o"], device_id_type=MESH)
        pl.semaphore_wait(barrier, 4)

    @pl.when(jnp.logical_not(middle))
    def _():
        pl.semaphore_wait(barrier, 3)

    def source(role, p, k):
        a, n = rows_of(p)
        if k == PLACE[role] and p in "AC":
            return tok.at[pl.ds(a, n)]
        return x.at[0, 0 if p in "AC" else 1, real(k), pl.ds(a, n)]

    def dispatch(role, d, p, k):
        a, n = rows_of(p)
        lane = 1 if d == "p" else 0
        q = {"A": "B", "C": "D"}[p] if d == "y" else p
        return pltpu.make_async_remote_copy(
            src_ref=source(role, p, k),
            dst_ref=x.at[lane, 0 if q in "AC" else 1, real(k), pl.ds(a, n)],
            send_sem=xs.at[DEST.index(d), 4 * LETTER.index(p) + k],
            recv_sem=xr.at[lane, 4 * LETTER.index(q) + real(k)],
            device_id=where[d],
            device_id_type=MESH,
        )

    def arrive(lane, p, k):
        a, n = rows_of(p)
        ref = x.at[lane, 0 if p in "AC" else 1, real(k), pl.ds(a, n)]
        pltpu.make_async_copy(ref, ref, xr.at[lane, 4 * LETTER.index(p) + real(k)]).wait()

    def z_slot(p, side, k):
        if p == "A":
            return rza.at[side, real(k)]
        return rzc.at[side, LETTER.index(p) - 2, real(k)]

    def z_sem(p, side, k):
        return rrz.at[side, 4 * LETTER.index(p) + real(k)]

    def give(role, p, k):
        unit = 4 * UNIT[p] + k
        a, n = held_rows(p)
        src = held.at[unit, pl.ds(a, n)]
        d = outgoing(role, p, k)
        if d == "f":
            first, count = rows_of(p)
            return pltpu.make_async_copy(src, out.at[pl.ds(first, count)], osem.at[0 if p == "A" else 1])
        if d == "y":
            dst, sem = (ry.at[real(k)], rry.at[real(k)]) if p == "B" else (ryc, rry.at[4])
        else:
            side = 1 if (d == "i" and role == 0) else 0
            dst, sem = z_slot(p, side, k), z_sem(p, side, k)
        return pltpu.make_async_remote_copy(
            src_ref=src, dst_ref=dst, send_sem=rs.at[4 * LETTER.index(p) + k], recv_sem=sem,
            device_id=where[d], device_id_type=MESH,
        )

    def settle(role, p, k, seen):
        unit = 4 * UNIT[p] + k
        a, n = held_rows(p)
        if ("P", unit) not in seen:
            seen.add(("P", unit))
            ref = pp.at[UNIT[p], real(k)]
            pltpu.make_async_copy(ref, ref, pr.at[UNIT[p], real(k)]).wait()
        refs = [pp.at[UNIT[p], real(k), pl.ds(a, n)]]
        for d in incoming(role, p, k):
            if d == "y":
                ref, sem = (ry.at[real(k)], rry.at[real(k)]) if p == "A" else (ryc, rry.at[4])
            else:
                side = 0 if d == "i" else 1
                ref, sem = z_slot(p, side, k), z_sem(p, side, k)
            pltpu.make_async_copy(ref, ref, sem).wait()
            refs.append(ref)
        loads = [pltpu.make_async_copy(ref, land.at[i, pl.ds(0, n)], isem.at[i]) for i, ref in enumerate(refs)]
        for copy in loads:
            copy.start()
        for copy in loads:
            copy.wait()
        wide = 1024 if width % 1024 == 0 else width

        @pl.loop(0, (n // 16) * (width // wide))
        def _(t):
            row = pl.multiple_of(t // (width // wide) * 16, 16)
            col = pl.multiple_of(t % (width // wide) * wide, wide)
            total = held[unit, pl.ds(a + row, 16), pl.ds(col, wide)].astype(jnp.float32)
            for i in range(len(refs)):
                total = total + land[i, pl.ds(row, 16), pl.ds(col, wide)].astype(jnp.float32)
            held[unit, pl.ds(a + row, 16), pl.ds(col, wide)] = total.astype(jnp.bfloat16)

        give(role, p, k).start()

    def load(role, u, k, seen):
        copies = []
        for j, p in enumerate("ABCD"):
            if UNIT[p] != u:
                continue
            a, n = rows_of(p)
            own = k == PLACE[role] and p in "AC"
            if not own and (0, p, k) not in seen:
                seen.add((0, p, k))
                arrive(0, p, k)
            arrive(1, p, k)
            at = PAIR // 2 if p == "D" else 0
            copies.append((source(role, p, k), at, n))
            copies.append((x.at[1, 0 if p in "AC" else 1, real(k), pl.ds(a, n)], PAIR + at, n))
        copies = [
            pltpu.make_async_copy(ref, left.at[pl.ds(at, n)], lsem.at[i]) for i, (ref, at, n) in enumerate(copies)
        ]
        for copy in copies:
            copy.start()
        for copy in copies:
            copy.wait()

    def act(role, action, seen):
        kind, p, k = action[0], action[-2], int(action[-1])
        if kind == "S":
            if not (k == PLACE[role] and p in "AC") and (0, p, k) not in seen:
                seen.add((0, p, k))
                arrive(0, p, k)
            dispatch(role, action[1], p, k).start()
        elif kind == "R":
            settle(role, p, k, seen)
        else:
            load(role, int(p), k, seen)

    segments, units = [], []
    for program in ORDER:
        parts, order = [[]], []
        for action in program:
            parts[-1].append(action)
            if action[0] == "C":
                order.append((int(action[-2]), int(action[-1])))
                parts.append([])
        segments.append(parts)
        units.append(order)
    steps = len(units[0])

    lane = lax.broadcasted_iota(jnp.int32, (2 * PAIR, SPAN), 1)
    chosen = (lane % 32 == me % experts) & (lane < 96)

    def multiply(step):
        kind, k = jnp.int32(0), jnp.int32(0)
        for i in range(steps):
            for role in (0, 1):
                hit = (step == i) & (middle if role else jnp.logical_not(middle))
                kind = jnp.where(hit, units[role][i][0], kind)
                k = jnp.where(hit, units[role][i][1], k)
        unit = 4 * kind + k
        slot = step % 2
        gates = jnp.where(chosen, left[:, width:].astype(jnp.float32), 0.0)
        gates = jnp.sum(gates, axis=1, keepdims=True)
        tile = 256

        @pl.loop(0, half // tile)
        def _(j):
            at = pl.multiple_of(j * tile, tile)
            gate = jnp.dot(left[:, :width], w1[:, pl.ds(at, tile)], preferred_element_type=jnp.float32)
            up = jnp.dot(left[:, :width], w1[:, pl.ds(half + at, tile)], preferred_element_type=jnp.float32)
            hid[:, pl.ds(at, tile)] = (gate / (1.0 + jnp.exp(-gate)) * up * gates).astype(jnp.bfloat16)

        back = pltpu.make_async_remote_copy(
            src_ref=ps.at[slot], dst_ref=pp.at[kind, real(k)], send_sem=ps_send.at[slot],
            recv_sem=pr.at[kind, real(k)], device_id=where["p"], device_id_type=MESH,
        )

        @pl.when(step >= 2)
        def _():
            back.wait_send()

        wide = 512 if width % 512 == 0 else width

        @pl.loop(0, width // wide)
        def _(j):
            at = pl.multiple_of(j * wide, wide)
            part = jnp.dot(hid[...], w2[:, pl.ds(at, wide)], preferred_element_type=jnp.float32)
            part = part.astype(jnp.bfloat16)
            held[unit, :, pl.ds(at, wide)] = part[:PAIR]
            ps[slot, :, pl.ds(at, wide)] = part[PAIR:]

        back.start()

    seen = [set(), set()]

    @pl.loop(0, steps)
    def _(step):
        for i in range(steps):
            for role in (0, 1):
                @pl.when((step == i) & (middle if role else jnp.logical_not(middle)))
                def _():
                    for action in segments[role][i]:
                        act(role, action, seen[role])

        @pl.when(step == 0)
        def _():
            for copy in weight_copies:
                copy.wait()

        multiply(step)

    for role in (0, 1):
        @pl.when(middle if role else jnp.logical_not(middle))
        def _():
            for action in segments[role][steps]:
                act(role, action, seen[role])
            for action in ORDER[role]:
                p, k = action[-2], int(action[-1])
                if action[0] == "S":
                    dispatch(role, action[1], p, k).wait_send()
                elif action[0] == "R":
                    if outgoing(role, p, k) == "f":
                        give(role, p, k).wait()
                    else:
                        give(role, p, k).wait_send()
    for slot in (0, 1):
        pltpu.make_async_remote_copy(
            src_ref=ps.at[slot], dst_ref=pp.at[0, 0], send_sem=ps_send.at[slot], recv_sem=pr.at[0, 0],
            device_id=where["p"], device_id_type=MESH,
        ).wait_send()


def fused(tokens, expert_ids, gate_weights, slot_expert, w_gate_up, w_down):
    devices = lax.axis_size("expert")
    experts = devices // 2
    rows, width = tokens.shape
    half = w_down.shape[1]
    chosen = expert_ids[:, :, None] == slot_expert[None, None, :experts]
    weights = jnp.sum(jnp.where(chosen, gate_weights[:, :, None], 0.0), axis=1)
    high = lax.reduce_precision(weights, 8, 7)
    mid = lax.reduce_precision(weights - high, 8, 7)
    low = weights - high - mid
    pad = jnp.zeros((rows, 32 - experts), jnp.float32)
    tail = jnp.concatenate([high, pad, mid, pad, low, pad, jnp.zeros((rows, 32), jnp.float32)], axis=1)
    wide = jnp.concatenate([tokens, tail.astype(jnp.bfloat16)], axis=1)
    full = width + SPAN
    bf16 = jnp.bfloat16
    rest = SPAN - HEAD
    shapes = [
        (rows, width),
        (2, 2, 4, rows, full),
        (3, 4, PAIR, width),
        (4, HEAD, width),
        (rest, width),
        (2, 4, HEAD, width),
        (2, 2, 4, rest, width),
    ]
    dma = pltpu.SemaphoreType.DMA
    results = pl.pallas_call(
        fused_kernel,
        out_shape=[jax.ShapeDtypeStruct(s, bf16) for s in shapes],
        in_specs=[pl.BlockSpec(memory_space=pl.ANY)] * 3,
        out_specs=[pl.BlockSpec(memory_space=pl.ANY)] * len(shapes),
        scratch_shapes=[
            pltpu.VMEM((width, 2 * half), bf16),
            pltpu.VMEM((half, width), bf16),
            pltpu.VMEM((2 * PAIR, full), bf16),
            pltpu.VMEM((2 * PAIR, half), bf16),
            pltpu.VMEM((12, PAIR, width), bf16),
            pltpu.VMEM((2, PAIR, width), bf16),
            pltpu.VMEM((4, HEAD, width), bf16),
            dma((2,)), dma((4,)), dma((4,)), dma((2,)),
            dma((4, 16)), dma((2, 16)), dma((2,)), dma((3, 4)), dma((16,)), dma((5,)), dma((2, 16)),
        ],
        compiler_params=pltpu.CompilerParams(
            collective_id=0, has_side_effects=True, vmem_limit_bytes=62 * 1024 * 1024
        ),
    )(wide, w_gate_up, w_down)
    return results[0]


def solution(mesh):
    return jax.shard_map(
        fused if mesh.shape["expert"] == 16 else per_device,
        mesh=mesh,
        in_specs=(
            P(("group", "expert"), None),
            P(("group", "expert"), None),
            P(("group", "expert"), None),
            P(),
            P("expert", None, None),
            P("expert", None, None),
        ),
        out_specs=P(("group", "expert"), None),
        check_vma=False,
    )
```

```python
import jax
import jax.numpy as jnp
import numpy as np
from jax import lax
from jax.experimental import pallas as pl
from jax.experimental.pallas import tpu as pltpu
from jax.sharding import PartitionSpec as P


def nearest(length):
    order = []
    for z in range(length):
        both = min(z, length - 1 - z)
        rest = [(t // 2 + 1, t % 2 == 0) for t in range(2 * both)]
        order.append(rest + [(t - both + 1, 2 * z > length - 1) for t in range(2 * both, length - 1)])
    return order


def pick(z, arrays, keys):
    out = arrays[keys[0]]
    for key in sorted(set(keys)):
        if key != keys[0]:
            hit = (z == np.array([i for i, k in enumerate(keys) if k == key])).any()
            out = jnp.where(hit, arrays[key], out)
    return out


def add(*terms):
    total = terms[0].astype(jnp.float32)
    for term in terms[1:]:
        total = total + term.astype(jnp.float32)
    return total.astype(jnp.bfloat16)


def per_device(tokens, expert_ids, gate_weights, slot_expert, w_gate_up, w_down):
    devices = lax.axis_size("expert")
    experts = devices // 2
    length = devices // 4
    rows, width = tokens.shape
    half = w_down.shape[1]
    me = lax.axis_index("expert")
    z, y, c = me // 4, me // 2 % 2, me % 2

    def line(x, step, who):
        return lax.ppermute(x, "expert", [(4 * i + j, 4 * (i + step) + j) for i in who for j in range(4)])

    def across(x):
        return lax.ppermute(x, "expert", [(i, i ^ 2) for i in range(devices)])

    def other_core(x):
        return lax.ppermute(x, "expert", [(i, i ^ 1) for i in range(devices)])

    chosen = expert_ids[:, :, None] == slot_expert[None, None, :experts]
    weights = jnp.sum(jnp.where(chosen, gate_weights[:, :, None], 0.0), axis=1)
    all_weights = lax.all_gather(weights, "expert", axis=0, tiled=False)
    mine = lax.dynamic_index_in_dim(all_weights, lax.rem(me, experts), axis=2, keepdims=False)

    order = nearest(length)
    mine, up, down = lax.optimization_barrier((mine, tokens, tokens))
    arrived, sums, chips = {}, {}, {}
    last = length - 2

    def halves(block, home):
        def rows_of(x, a):
            gates = jnp.concatenate([mine[4 * home + 2 * a + b] for b in (c, 1 - c)])
            return jnp.concatenate([x, other_core(x)], axis=0), gates[:, None]
        return rows_of(block, y), rows_of(across(block), 1 - y)

    def expert(parts):
        group = jnp.concatenate([part[0] for part in parts], axis=0)
        w = jnp.concatenate([part[1] for part in parts], axis=0)
        projected = jnp.dot(group, w_gate_up[0], preferred_element_type=jnp.float32)
        hidden = (jax.nn.silu(projected[:, :half]) * projected[:, half:]).astype(jnp.bfloat16)
        partial = (jnp.dot(hidden, w_down[0], preferred_element_type=jnp.float32) * w).astype(jnp.bfloat16)
        out = []
        for i in range(len(parts)):
            own = partial[2 * i * rows:(2 * i + 1) * rows]
            out.append(add(own, other_core(partial[(2 * i + 1) * rows:(2 * i + 2) * rows])))
        return out

    waiting, names = list(halves(tokens, z)), [(-1, 0), (-1, 1)]
    for s in range(1, length):
        up = line(up, 1, range(s - 1, length - 1))
        down = line(down, -1, range(1, length - s + 1))
        arrived[(s, True)], arrived[(s, False)] = up, down
        t = s - 1
        block = pick(z, arrived, [order[i][t] for i in range(length)])
        if t < last:
            block, up, down = lax.optimization_barrier((block, up, down))
        elif (-1, 0) in chips:
            block, chips[(-1, 0)] = lax.optimization_barrier((block, chips[(-1, 0)]))
        home = jnp.asarray([i - order[i][t][0] * (1 if order[i][t][1] else -1) for i in range(length)], jnp.int32)[z]
        near, far = halves(block, home)
        waiting.append(near)
        names.append((t, 0))
        if t < last:
            waiting.append(far)
            names.append((t, 1))
        if t != last - 1:
            chips.update(zip(names, expert(waiting)))
            waiting, names = [], []
    chips.update(zip([(last, 1)], expert([far])))
    index = [{(s, d): t for t, (s, d) in enumerate(order[i])} for i in range(length)]
    rising = {s: [index[i].get((s, False), last) for i in range(length)] for s in range(1, length)}
    falling = {s: [index[i].get((s, True), last) for i in range(length)] for s in range(1, length)}
    got, picked = None, {}

    def settle(t, got):
        sums[t] = add(chips[(t, 0)], got)
        ready = [s for s in rising if s not in picked and set(rising[s] + falling[s]) <= set(sums)]
        for s in reversed(ready):
            picked[s] = lax.optimization_barrier((pick(z, sums, rising[s]), pick(z, sums, falling[s])))
        return ready

    for t in [last - 1, last] + list(range(last - 2, -2, -1)):
        leave = chips[(t, 1)]
        if got is not None:
            leave, got = lax.optimization_barrier((leave, got))
            for s in settle(before, got):
                leave, picked[s] = lax.optimization_barrier((leave, picked[s]))
        got, before = across(leave), t
    settle(before, got)
    from_below = from_above = None
    for s in reversed(range(1, length)):
        rise, fall = picked[s]
        if from_below is not None:
            rise, fall = add(rise, from_below), add(fall, from_above)
        from_below = line(rise, 1, range(0, length - s))
        from_above = line(fall, -1, range(s, length))
    return add(sums[-1], from_below, from_above)


ORDER = (
    (
        "SiE0", "SpC0", "SyC0", "SpE0", "SpA0", "SiC0", "C00", "SpE1", "SyE1", "SpD0", "SiA0", "SyE0",
        "SpA1", "C20", "SpF1", "SiD0", "SyA1", "C01", "SpC2", "SpF0", "SyA0", "SpE3", "SpB1", "SyE3",
        "C11", "SpD2", "SpB0", "RF1", "SpF3", "C22", "SpC3", "RB1", "RE1", "C10", "SyA3", "SpA3",
        "RD2", "C03", "SpD3", "RA1", "RB0", "SpB3", "SpE2", "C23", "SyE2", "RC2", "SpA2", "C13",
        "SyA2", "RC3", "SpF2", "C02", "SpC1", "RF3", "RD3", "SpB2", "RB3", "SpD1", "C12", "RE3",
        "C21", "RB2", "RA3", "RF2", "RD1", "RF0", "RA2", "RD0", "RE2", "RE0", "RC1", "RC0",
        "RA0",
    ),
    (
        "SpC1", "SoE1", "SyC1", "SiC1", "SpA1", "SpE1", "SoA1", "C01", "SiE0", "SpE0", "SpD1", "SpC2",
        "SyE1", "SoC2", "SiD1", "SyE0", "SpC0", "C21", "SiC0", "SoE3", "SpE3", "SyE3", "SpF1", "SpF0",
        "SyA1", "SpA0", "SpD2", "SoD2", "SpF3", "SiA0", "C00", "SoC3", "SpD0", "SyA0", "SpC3", "C22",
        "SiD0", "SpB1", "C20", "SoA3", "SpA3", "SyA3", "SpB0", "C11", "SiE1", "SpD3", "SoD3", "C03",
        "SpB3", "SiA1", "RF1", "C23", "SoE2", "SpE2", "SyE2", "C13", "SyA2", "SpA2", "SoA2", "C10",
        "SpF2", "RD2", "RB3", "SoC1", "C02", "SpB2", "RB0", "SoD1", "C12", "RC2", "RF3", "RF2",
        "RC3", "RB2", "RD3", "RC0", "RB1", "RE3", "RD0", "RF0", "RA3", "RD1", "RE0", "RA0",
        "RA2", "RE2", "RA1", "RC1", "RE1",
    ),
)


HEAD, SPAN = 80, 128
FIRST = 48
PAIR = 96
MESH = pl.DeviceIdType.MESH
PLACE = (0, 1)
UNIT = {"A": 0, "E": 0, "B": 1, "F": 1, "C": 2, "D": 2}
LETTER = "ABCDEF"
OWN = "ACE"
FLIP = {"A": "B", "E": "F", "C": "D"}


def incoming(role, p, k):
    if p in "BF":
        return []
    at = PLACE[role]
    if k == at:
        got = ["i", "o"] if role else ["i"]
    elif k > at:
        got = ["o"] if role else []
    else:
        got = ["i"]
    if p in "AE" or (p == "C" and k == at):
        got = got + ["y"]
    return got


def outgoing(role, p, k):
    if p in "BF":
        return "y"
    at = PLACE[role]
    if k == at:
        return "f" if p in OWN else "y"
    return "o" if k < at else "i"


def rows_of(p):
    if p in "AB":
        return 0, FIRST
    return (FIRST, HEAD - FIRST) if p in "EF" else (HEAD, SPAN - HEAD)


def held_rows(p):
    if p in "CD":
        return (0 if p == "C" else PAIR // 2), SPAN - HEAD
    return rows_of(p)


def fused_kernel(tok, w1_any, w2_any, out, x, pp, ry, ryc, rza, rzc, w1, w2, left, hid, held, ps, land,
                 wsem, lsem, isem, osem, xs, xr, ps_send, pr, rs, rry, rrz):
    width = w2.shape[1]
    half = w2.shape[0]
    experts = lax.axis_size("expert") // 2
    me = lax.axis_index("expert")
    z, y, c = me // 4, me // 2 % 2, me % 2
    low = z < 2
    middle = (z == 1) | (z == 2)
    inner = jnp.where(low, z + 1, z - 1)
    outer = jnp.where(low, jnp.maximum(z - 1, 0), jnp.minimum(z + 1, 3))
    where = {
        "i": {"expert": 4 * inner + 2 * y + c},
        "o": {"expert": 4 * outer + 2 * y + c},
        "y": {"expert": 4 * z + 2 * (1 - y) + c},
        "p": {"expert": 4 * z + 2 * y + 1 - c},
    }
    DEST = "ioyp"

    def real(k):
        return jnp.where(low, k, 3 - k)

    weight_copies = [
        pltpu.make_async_copy(w1_any.at[0], w1, wsem.at[0]),
        pltpu.make_async_copy(w2_any.at[0], w2, wsem.at[1]),
    ]
    for copy in weight_copies:
        copy.start()

    barrier = pltpu.get_barrier_semaphore()
    for d in "iyp":
        pl.semaphore_signal(barrier, inc=1, device_id=where[d], device_id_type=MESH)

    @pl.when(middle)
    def _():
        pl.semaphore_signal(barrier, inc=1, device_id=where["o"], device_id_type=MESH)
        pl.semaphore_wait(barrier, 4)

    @pl.when(jnp.logical_not(middle))
    def _():
        pl.semaphore_wait(barrier, 3)

    def source(role, p, k):
        a, n = rows_of(p)
        if k == PLACE[role] and p in OWN:
            return tok.at[pl.ds(a, n)]
        return x.at[0, 0 if p in OWN else 1, real(k), pl.ds(a, n)]

    def dispatch(role, d, p, k):
        a, n = rows_of(p)
        lane = 1 if d == "p" else 0
        q = FLIP[p] if d == "y" else p
        return pltpu.make_async_remote_copy(
            src_ref=source(role, p, k),
            dst_ref=x.at[lane, 0 if q in OWN else 1, real(k), pl.ds(a, n)],
            send_sem=xs.at[DEST.index(d), 4 * LETTER.index(p) + k],
            recv_sem=xr.at[lane, 4 * LETTER.index(q) + real(k)],
            device_id=where[d],
            device_id_type=MESH,
        )

    def arrive(lane, p, k):
        a, n = rows_of(p)
        ref = x.at[lane, 0 if p in OWN else 1, real(k), pl.ds(a, n)]
        pltpu.make_async_copy(ref, ref, xr.at[lane, 4 * LETTER.index(p) + real(k)]).wait()

    def z_slot(p, side, k):
        if p in "AE":
            a, n = rows_of(p)
            return rza.at[side, real(k), pl.ds(a, n)]
        return rzc.at[side, LETTER.index(p) - 2, real(k)]

    def y_slot(p, k):
        a, n = rows_of(p)
        if p in "CD":
            return ryc, rry.at[8]
        return ry.at[real(k), pl.ds(a, n)], rry.at[(4 if p in "EF" else 0) + real(k)]

    def z_sem(p, side, k):
        return rrz.at[side, 4 * LETTER.index(p) + real(k)]

    def give(role, p, k):
        unit = 4 * UNIT[p] + k
        a, n = held_rows(p)
        src = held.at[unit, pl.ds(a, n)]
        d = outgoing(role, p, k)
        if d == "f":
            first, count = rows_of(p)
            return pltpu.make_async_copy(src, out.at[pl.ds(first, count)], osem.at[LETTER.index(p) // 2])
        if d == "y":
            dst, sem = y_slot(p, k)
        else:
            side = 1 if (d == "i" and role == 0) else 0
            dst, sem = z_slot(p, side, k), z_sem(p, side, k)
        return pltpu.make_async_remote_copy(
            src_ref=src, dst_ref=dst, send_sem=rs.at[4 * LETTER.index(p) + k], recv_sem=sem,
            device_id=where[d], device_id_type=MESH,
        )

    def settle(role, p, k, seen):
        unit = 4 * UNIT[p] + k
        a, n = held_rows(p)
        if ("P", unit) not in seen:
            seen.add(("P", unit))
            ref = pp.at[UNIT[p], real(k)]
            pltpu.make_async_copy(ref, ref, pr.at[UNIT[p], real(k)]).wait()
        refs = [pp.at[UNIT[p], real(k), pl.ds(a, n)]]
        for d in incoming(role, p, k):
            if d == "y":
                ref, sem = y_slot(p, k)
            else:
                side = 0 if d == "i" else 1
                ref, sem = z_slot(p, side, k), z_sem(p, side, k)
            pltpu.make_async_copy(ref, ref, sem).wait()
            refs.append(ref)
        loads = [pltpu.make_async_copy(ref, land.at[i, pl.ds(0, n)], isem.at[i]) for i, ref in enumerate(refs)]
        for copy in loads:
            copy.start()
        for copy in loads:
            copy.wait()
        wide = 1024 if width % 1024 == 0 else width

        @pl.loop(0, (n // 16) * (width // wide))
        def _(t):
            row = pl.multiple_of(t // (width // wide) * 16, 16)
            col = pl.multiple_of(t % (width // wide) * wide, wide)
            total = held[unit, pl.ds(a + row, 16), pl.ds(col, wide)].astype(jnp.float32)
            for i in range(len(refs)):
                total = total + land[i, pl.ds(row, 16), pl.ds(col, wide)].astype(jnp.float32)
            held[unit, pl.ds(a + row, 16), pl.ds(col, wide)] = total.astype(jnp.bfloat16)

        give(role, p, k).start()

    def load(role, u, k, seen):
        copies = []
        for p in LETTER:
            if UNIT[p] != u:
                continue
            a, n = rows_of(p)
            own = k == PLACE[role] and p in OWN
            if not own and (0, p, k) not in seen:
                seen.add((0, p, k))
                arrive(0, p, k)
            arrive(1, p, k)
            at = held_rows(p)[0]
            copies.append((source(role, p, k), at, n))
            copies.append((x.at[1, 0 if p in OWN else 1, real(k), pl.ds(a, n)], PAIR + at, n))
        copies = [
            pltpu.make_async_copy(ref, left.at[pl.ds(at, n)], lsem.at[i]) for i, (ref, at, n) in enumerate(copies)
        ]
        for copy in copies:
            copy.start()
        for copy in copies:
            copy.wait()

    def act(role, action, seen):
        kind, p, k = action[0], action[-2], int(action[-1])
        if kind == "S":
            if not (k == PLACE[role] and p in OWN) and (0, p, k) not in seen:
                seen.add((0, p, k))
                arrive(0, p, k)
            dispatch(role, action[1], p, k).start()
        elif kind == "R":
            settle(role, p, k, seen)
        else:
            load(role, int(p), k, seen)

    segments, units = [], []
    for program in ORDER:
        parts, order = [[]], []
        for action in program:
            parts[-1].append(action)
            if action[0] == "C":
                order.append((int(action[-2]), int(action[-1])))
                parts.append([])
        segments.append(parts)
        units.append(order)
    steps = len(units[0])

    lane = lax.broadcasted_iota(jnp.int32, (2 * PAIR, SPAN), 1)
    chosen = (lane % 32 == me % experts) & (lane < 96)

    def multiply(step):
        kind, k = jnp.int32(0), jnp.int32(0)
        for i in range(steps):
            for role in (0, 1):
                hit = (step == i) & (middle if role else jnp.logical_not(middle))
                kind = jnp.where(hit, units[role][i][0], kind)
                k = jnp.where(hit, units[role][i][1], k)
        unit = 4 * kind + k
        slot = step % 2
        gates = jnp.where(chosen, left[:, width:].astype(jnp.float32), 0.0)
        gates = jnp.sum(gates, axis=1, keepdims=True)
        tile = 256

        @pl.loop(0, half // tile)
        def _(j):
            at = pl.multiple_of(j * tile, tile)
            gate = jnp.dot(left[:, :width], w1[:, pl.ds(at, tile)], preferred_element_type=jnp.float32)
            up = jnp.dot(left[:, :width], w1[:, pl.ds(half + at, tile)], preferred_element_type=jnp.float32)
            hid[:, pl.ds(at, tile)] = (gate / (1.0 + jnp.exp(-gate)) * up * gates).astype(jnp.bfloat16)

        back = pltpu.make_async_remote_copy(
            src_ref=ps.at[slot], dst_ref=pp.at[kind, real(k)], send_sem=ps_send.at[slot],
            recv_sem=pr.at[kind, real(k)], device_id=where["p"], device_id_type=MESH,
        )

        @pl.when(step >= 2)
        def _():
            back.wait_send()

        wide = 512 if width % 512 == 0 else width

        @pl.loop(0, width // wide)
        def _(j):
            at = pl.multiple_of(j * wide, wide)
            part = jnp.dot(hid[...], w2[:, pl.ds(at, wide)], preferred_element_type=jnp.float32)
            part = part.astype(jnp.bfloat16)
            held[unit, :, pl.ds(at, wide)] = part[:PAIR]
            ps[slot, :, pl.ds(at, wide)] = part[PAIR:]

        back.start()

    seen = [set(), set()]

    @pl.loop(0, steps)
    def _(step):
        for i in range(steps):
            for role in (0, 1):
                @pl.when((step == i) & (middle if role else jnp.logical_not(middle)))
                def _():
                    for action in segments[role][i]:
                        act(role, action, seen[role])

        @pl.when(step == 0)
        def _():
            for copy in weight_copies:
                copy.wait()

        multiply(step)

    for role in (0, 1):
        @pl.when(middle if role else jnp.logical_not(middle))
        def _():
            for action in segments[role][steps]:
                act(role, action, seen[role])
            for action in ORDER[role]:
                p, k = action[-2], int(action[-1])
                if action[0] == "S":
                    dispatch(role, action[1], p, k).wait_send()
                elif action[0] == "R":
                    if outgoing(role, p, k) == "f":
                        give(role, p, k).wait()
                    else:
                        give(role, p, k).wait_send()
    for slot in (0, 1):
        pltpu.make_async_remote_copy(
            src_ref=ps.at[slot], dst_ref=pp.at[0, 0], send_sem=ps_send.at[slot], recv_sem=pr.at[0, 0],
            device_id=where["p"], device_id_type=MESH,
        ).wait_send()


def fused(tokens, expert_ids, gate_weights, slot_expert, w_gate_up, w_down):
    devices = lax.axis_size("expert")
    experts = devices // 2
    rows, width = tokens.shape
    half = w_down.shape[1]
    chosen = expert_ids[:, :, None] == slot_expert[None, None, :experts]
    weights = jnp.sum(jnp.where(chosen, gate_weights[:, :, None], 0.0), axis=1)
    high = lax.reduce_precision(weights, 8, 7)
    mid = lax.reduce_precision(weights - high, 8, 7)
    low = weights - high - mid
    pad = jnp.zeros((rows, 32 - experts), jnp.float32)
    tail = jnp.concatenate([high, pad, mid, pad, low, pad, jnp.zeros((rows, 32), jnp.float32)], axis=1)
    wide = jnp.concatenate([tokens, tail.astype(jnp.bfloat16)], axis=1)
    full = width + SPAN
    bf16 = jnp.bfloat16
    rest = SPAN - HEAD
    shapes = [
        (rows, width),
        (2, 2, 4, rows, full),
        (3, 4, PAIR, width),
        (4, HEAD, width),
        (rest, width),
        (2, 4, HEAD, width),
        (2, 2, 4, rest, width),
    ]
    dma = pltpu.SemaphoreType.DMA
    results = pl.pallas_call(
        fused_kernel,
        out_shape=[jax.ShapeDtypeStruct(s, bf16) for s in shapes],
        in_specs=[pl.BlockSpec(memory_space=pl.ANY)] * 3,
        out_specs=[pl.BlockSpec(memory_space=pl.ANY)] * len(shapes),
        scratch_shapes=[
            pltpu.VMEM((width, 2 * half), bf16),
            pltpu.VMEM((half, width), bf16),
            pltpu.VMEM((2 * PAIR, full), bf16),
            pltpu.VMEM((2 * PAIR, half), bf16),
            pltpu.VMEM((12, PAIR, width), bf16),
            pltpu.VMEM((2, PAIR, width), bf16),
            pltpu.VMEM((4, FIRST, width), bf16),
            dma((2,)), dma((4,)), dma((4,)), dma((3,)),
            dma((4, 24)), dma((2, 24)), dma((2,)), dma((3, 4)), dma((24,)), dma((9,)), dma((2, 24)),
        ],
        compiler_params=pltpu.CompilerParams(
            collective_id=0, has_side_effects=True, vmem_limit_bytes=62 * 1024 * 1024
        ),
    )(wide, w_gate_up, w_down)
    return results[0]


def solution(mesh):
    return jax.shard_map(
        fused if mesh.shape["expert"] == 16 else per_device,
        mesh=mesh,
        in_specs=(
            P(("group", "expert"), None),
            P(("group", "expert"), None),
            P(("group", "expert"), None),
            P(),
            P("expert", None, None),
            P("expert", None, None),
        ),
        out_specs=P(("group", "expert"), None),
        check_vma=False,
    )
```

```python
import jax
import jax.numpy as jnp
import numpy as np
from jax import lax
from jax.experimental import pallas as pl
from jax.experimental.pallas import tpu as pltpu
from jax.sharding import PartitionSpec as P


def nearest(length):
    order = []
    for z in range(length):
        both = min(z, length - 1 - z)
        rest = [(t // 2 + 1, t % 2 == 0) for t in range(2 * both)]
        order.append(rest + [(t - both + 1, 2 * z > length - 1) for t in range(2 * both, length - 1)])
    return order


def pick(z, arrays, keys):
    out = arrays[keys[0]]
    for key in sorted(set(keys)):
        if key != keys[0]:
            hit = (z == np.array([i for i, k in enumerate(keys) if k == key])).any()
            out = jnp.where(hit, arrays[key], out)
    return out


def add(*terms):
    total = terms[0].astype(jnp.float32)
    for term in terms[1:]:
        total = total + term.astype(jnp.float32)
    return total.astype(jnp.bfloat16)


def per_device(tokens, expert_ids, gate_weights, slot_expert, w_gate_up, w_down):
    devices = lax.axis_size("expert")
    experts = devices // 2
    length = devices // 4
    rows, width = tokens.shape
    half = w_down.shape[1]
    me = lax.axis_index("expert")
    z, y, c = me // 4, me // 2 % 2, me % 2

    def line(x, step, who):
        return lax.ppermute(x, "expert", [(4 * i + j, 4 * (i + step) + j) for i in who for j in range(4)])

    def across(x):
        return lax.ppermute(x, "expert", [(i, i ^ 2) for i in range(devices)])

    def other_core(x):
        return lax.ppermute(x, "expert", [(i, i ^ 1) for i in range(devices)])

    chosen = expert_ids[:, :, None] == slot_expert[None, None, :experts]
    weights = jnp.sum(jnp.where(chosen, gate_weights[:, :, None], 0.0), axis=1)
    all_weights = lax.all_gather(weights, "expert", axis=0, tiled=False)
    mine = lax.dynamic_index_in_dim(all_weights, lax.rem(me, experts), axis=2, keepdims=False)

    order = nearest(length)
    mine, up, down = lax.optimization_barrier((mine, tokens, tokens))
    arrived, sums, chips = {}, {}, {}
    last = length - 2

    def halves(block, home):
        def rows_of(x, a):
            gates = jnp.concatenate([mine[4 * home + 2 * a + b] for b in (c, 1 - c)])
            return jnp.concatenate([x, other_core(x)], axis=0), gates[:, None]
        return rows_of(block, y), rows_of(across(block), 1 - y)

    def expert(parts):
        group = jnp.concatenate([part[0] for part in parts], axis=0)
        w = jnp.concatenate([part[1] for part in parts], axis=0)
        projected = jnp.dot(group, w_gate_up[0], preferred_element_type=jnp.float32)
        hidden = (jax.nn.silu(projected[:, :half]) * projected[:, half:]).astype(jnp.bfloat16)
        partial = (jnp.dot(hidden, w_down[0], preferred_element_type=jnp.float32) * w).astype(jnp.bfloat16)
        out = []
        for i in range(len(parts)):
            own = partial[2 * i * rows:(2 * i + 1) * rows]
            out.append(add(own, other_core(partial[(2 * i + 1) * rows:(2 * i + 2) * rows])))
        return out

    waiting, names = list(halves(tokens, z)), [(-1, 0), (-1, 1)]
    for s in range(1, length):
        up = line(up, 1, range(s - 1, length - 1))
        down = line(down, -1, range(1, length - s + 1))
        arrived[(s, True)], arrived[(s, False)] = up, down
        t = s - 1
        block = pick(z, arrived, [order[i][t] for i in range(length)])
        if t < last:
            block, up, down = lax.optimization_barrier((block, up, down))
        elif (-1, 0) in chips:
            block, chips[(-1, 0)] = lax.optimization_barrier((block, chips[(-1, 0)]))
        home = jnp.asarray([i - order[i][t][0] * (1 if order[i][t][1] else -1) for i in range(length)], jnp.int32)[z]
        near, far = halves(block, home)
        waiting.append(near)
        names.append((t, 0))
        if t < last:
            waiting.append(far)
            names.append((t, 1))
        if t != last - 1:
            chips.update(zip(names, expert(waiting)))
            waiting, names = [], []
    chips.update(zip([(last, 1)], expert([far])))
    index = [{(s, d): t for t, (s, d) in enumerate(order[i])} for i in range(length)]
    rising = {s: [index[i].get((s, False), last) for i in range(length)] for s in range(1, length)}
    falling = {s: [index[i].get((s, True), last) for i in range(length)] for s in range(1, length)}
    got, picked = None, {}

    def settle(t, got):
        sums[t] = add(chips[(t, 0)], got)
        ready = [s for s in rising if s not in picked and set(rising[s] + falling[s]) <= set(sums)]
        for s in reversed(ready):
            picked[s] = lax.optimization_barrier((pick(z, sums, rising[s]), pick(z, sums, falling[s])))
        return ready

    for t in [last - 1, last] + list(range(last - 2, -2, -1)):
        leave = chips[(t, 1)]
        if got is not None:
            leave, got = lax.optimization_barrier((leave, got))
            for s in settle(before, got):
                leave, picked[s] = lax.optimization_barrier((leave, picked[s]))
        got, before = across(leave), t
    settle(before, got)
    from_below = from_above = None
    for s in reversed(range(1, length)):
        rise, fall = picked[s]
        if from_below is not None:
            rise, fall = add(rise, from_below), add(fall, from_above)
        from_below = line(rise, 1, range(0, length - s))
        from_above = line(fall, -1, range(s, length))
    return add(sums[-1], from_below, from_above)


ORDER = (
    (
        "SyC0", "SiE0", "SpA0", "SpC0", "SpE0", "SiA0", "C00", "SyE1", "SpE1", "SpD0", "SiD0", "SyA0",
        "SpA1", "C20", "SpF1", "C01", "SiC0", "SyA1", "SpC2", "SpB0", "SyE0", "SpE3", "SpB1", "SyE3",
        "C11", "SpF0", "SpD2", "RF1", "C10", "SyA3", "SpA3", "SpF3", "C22", "RE1", "C03", "SpD3",
        "RB1", "RC2", "SpB3", "RB0", "SpC3", "RD2", "C13", "C23", "SyA2", "SpA2", "RA1", "SpE2",
        "C02", "SyE2", "RD3", "SpB2", "RB3", "SpC1", "RC3", "SpF2", "C12", "SpD1", "RF3", "RA3",
        "RF0", "C21", "RB2", "RE3", "RD1", "RF2", "RD0", "RA2", "RE2", "RA0", "RC0", "RC1",
        "RE0",
    ),
    (
        "SoE1", "SiC1", "SyC1", "SpC1", "SpA1", "SpE1", "SoA1", "C01", "SiE0", "SyE0", "SpE0", "SpC2",
        "SpD1", "SoC2", "SiD1", "SyA1", "SpA0", "SpE3", "SpF0", "C21", "SiA0", "SoE3", "SyA0", "C00",
        "SpD2", "SpD0", "SpB1", "SoD2", "SiD0", "SyE3", "C22", "SpC0", "SpA3", "SoA3", "SyA3", "SpB0",
        "SiC0", "SpF3", "C20", "SoD3", "SpD3", "SyE1", "C03", "SpB3", "SiA1", "C10", "SoC3", "SpC3",
        "SpF1", "C13", "SiE1", "RF0", "C23", "SoA2", "SyA2", "SpA2", "C11", "SpE2", "SoE2", "RC2",
        "SyE2", "C02", "SpB2", "SoC1", "RB3", "RD2", "SpF2", "C12", "SoD1", "RB1", "RF3", "RD3",
        "RB0", "RC3", "RD0", "RB2", "RA3", "RC0", "RF1", "RE3", "RF2", "RA0", "RD1", "RE0",
        "RA2", "RE2", "RA1", "RC1", "RE1",
    ),
)


HEAD, SPAN = 80, 128
FIRST = 48
PAIR = 96
MESH = pl.DeviceIdType.MESH
PLACE = (0, 1)
UNIT = {"A": 0, "E": 0, "B": 1, "F": 1, "C": 2, "D": 2}
LETTER = "ABCDEF"
OWN = "ACE"
FLIP = {"A": "B", "E": "F", "C": "D"}


def incoming(role, p, k):
    if p in "BF":
        return []
    at = PLACE[role]
    if k == at:
        got = ["i", "o"] if role else ["i"]
    elif k > at:
        got = ["o"] if role else []
    else:
        got = ["i"]
    if p in "AE" or (p == "C" and k == at):
        got = got + ["y"]
    return got


def outgoing(role, p, k):
    if p in "BF":
        return "y"
    at = PLACE[role]
    if k == at:
        return "f" if p in OWN else "y"
    return "o" if k < at else "i"


def rows_of(p):
    if p in "AB":
        return 0, FIRST
    return (FIRST, HEAD - FIRST) if p in "EF" else (HEAD, SPAN - HEAD)


def held_rows(p):
    if p in "CD":
        return (0 if p == "C" else PAIR // 2), SPAN - HEAD
    return rows_of(p)


def fused_kernel(tok, w1_any, w2_any, out, x, pp, ry, ryc, rza, rzc, w1, w2, left, hid, held, ps, land,
                 wsem, lsem, isem, osem, xs, xr, ps_send, pr, rs, rry, rrz):
    width = w2.shape[1]
    half = w2.shape[0]
    experts = lax.axis_size("expert") // 2
    me = lax.axis_index("expert")
    z, y, c = me // 4, me // 2 % 2, me % 2
    low = z < 2
    middle = (z == 1) | (z == 2)
    inner = jnp.where(low, z + 1, z - 1)
    outer = jnp.where(low, jnp.maximum(z - 1, 0), jnp.minimum(z + 1, 3))
    where = {
        "i": {"expert": 4 * inner + 2 * y + c},
        "o": {"expert": 4 * outer + 2 * y + c},
        "y": {"expert": 4 * z + 2 * (1 - y) + c},
        "p": {"expert": 4 * z + 2 * y + 1 - c},
    }
    DEST = "ioyp"

    def real(k):
        return jnp.where(low, k, 3 - k)

    weight_copies = [
        pltpu.make_async_copy(w1_any.at[0], w1, wsem.at[0]),
        pltpu.make_async_copy(w2_any.at[0], w2, wsem.at[1]),
    ]
    for copy in weight_copies:
        copy.start()

    barrier = pltpu.get_barrier_semaphore()
    for d in "iyp":
        pl.semaphore_signal(barrier, inc=1, device_id=where[d], device_id_type=MESH)

    @pl.when(middle)
    def _():
        pl.semaphore_signal(barrier, inc=1, device_id=where["o"], device_id_type=MESH)
        pl.semaphore_wait(barrier, 4)

    @pl.when(jnp.logical_not(middle))
    def _():
        pl.semaphore_wait(barrier, 3)

    def source(role, p, k):
        a, n = rows_of(p)
        if k == PLACE[role] and p in OWN:
            return tok.at[pl.ds(a, n)]
        return x.at[0, 0 if p in OWN else 1, real(k), pl.ds(a, n)]

    def dispatch(role, d, p, k):
        a, n = rows_of(p)
        lane = 1 if d == "p" else 0
        q = FLIP[p] if d == "y" else p
        return pltpu.make_async_remote_copy(
            src_ref=source(role, p, k),
            dst_ref=x.at[lane, 0 if q in OWN else 1, real(k), pl.ds(a, n)],
            send_sem=xs.at[DEST.index(d), 4 * LETTER.index(p) + k],
            recv_sem=xr.at[lane, 4 * LETTER.index(q) + real(k)],
            device_id=where[d],
            device_id_type=MESH,
        )

    def arrive(lane, p, k):
        a, n = rows_of(p)
        ref = x.at[lane, 0 if p in OWN else 1, real(k), pl.ds(a, n)]
        pltpu.make_async_copy(ref, ref, xr.at[lane, 4 * LETTER.index(p) + real(k)]).wait()

    def z_slot(p, side, k):
        if p in "AE":
            a, n = rows_of(p)
            return rza.at[side, real(k), pl.ds(a, n)]
        return rzc.at[side, LETTER.index(p) - 2, real(k)]

    def y_slot(p, k):
        a, n = rows_of(p)
        if p in "CD":
            return ryc, rry.at[8]
        return ry.at[real(k), pl.ds(a, n)], rry.at[(4 if p in "EF" else 0) + real(k)]

    def z_sem(p, side, k):
        return rrz.at[side, 4 * LETTER.index(p) + real(k)]

    def give(role, p, k):
        unit = 4 * UNIT[p] + k
        a, n = held_rows(p)
        src = held.at[unit, pl.ds(a, n)]
        d = outgoing(role, p, k)
        if d == "f":
            first, count = rows_of(p)
            return pltpu.make_async_copy(src, out.at[pl.ds(first, count)], osem.at[LETTER.index(p) // 2])
        if d == "y":
            dst, sem = y_slot(p, k)
        else:
            side = 1 if (d == "i" and role == 0) else 0
            dst, sem = z_slot(p, side, k), z_sem(p, side, k)
        return pltpu.make_async_remote_copy(
            src_ref=src, dst_ref=dst, send_sem=rs.at[4 * LETTER.index(p) + k], recv_sem=sem,
            device_id=where[d], device_id_type=MESH,
        )

    def settle(role, p, k, seen):
        unit = 4 * UNIT[p] + k
        a, n = held_rows(p)
        if ("P", unit) not in seen:
            seen.add(("P", unit))
            ref = pp.at[UNIT[p], real(k)]
            pltpu.make_async_copy(ref, ref, pr.at[UNIT[p], real(k)]).wait()
        refs = [pp.at[UNIT[p], real(k), pl.ds(a, n)]]
        for d in incoming(role, p, k):
            if d == "y":
                ref, sem = y_slot(p, k)
            else:
                side = 0 if d == "i" else 1
                ref, sem = z_slot(p, side, k), z_sem(p, side, k)
            pltpu.make_async_copy(ref, ref, sem).wait()
            refs.append(ref)
        loads = [pltpu.make_async_copy(ref, land.at[i, pl.ds(0, n)], isem.at[i]) for i, ref in enumerate(refs)]
        for copy in loads:
            copy.start()
        for copy in loads:
            copy.wait()
        wide = 1024 if width % 1024 == 0 else width

        @pl.loop(0, (n // 16) * (width // wide))
        def _(t):
            row = pl.multiple_of(t // (width // wide) * 16, 16)
            col = pl.multiple_of(t % (width // wide) * wide, wide)
            total = held[unit, pl.ds(a + row, 16), pl.ds(col, wide)].astype(jnp.float32)
            for i in range(len(refs)):
                total = total + land[i, pl.ds(row, 16), pl.ds(col, wide)].astype(jnp.float32)
            held[unit, pl.ds(a + row, 16), pl.ds(col, wide)] = total.astype(jnp.bfloat16)

        give(role, p, k).start()

    def load(role, u, k, seen):
        copies = []
        for p in LETTER:
            if UNIT[p] != u:
                continue
            a, n = rows_of(p)
            own = k == PLACE[role] and p in OWN
            if not own and (0, p, k) not in seen:
                seen.add((0, p, k))
                arrive(0, p, k)
            arrive(1, p, k)
            at = held_rows(p)[0]
            copies.append((source(role, p, k), at, n))
            copies.append((x.at[1, 0 if p in OWN else 1, real(k), pl.ds(a, n)], PAIR + at, n))
        copies = [
            pltpu.make_async_copy(ref, left.at[pl.ds(at, n)], lsem.at[i]) for i, (ref, at, n) in enumerate(copies)
        ]
        for copy in copies:
            copy.start()
        for copy in copies:
            copy.wait()

    def act(role, action, seen):
        kind, p, k = action[0], action[-2], int(action[-1])
        if kind == "S":
            if not (k == PLACE[role] and p in OWN) and (0, p, k) not in seen:
                seen.add((0, p, k))
                arrive(0, p, k)
            dispatch(role, action[1], p, k).start()
        elif kind == "R":
            settle(role, p, k, seen)
        else:
            load(role, int(p), k, seen)

    segments, units = [], []
    for program in ORDER:
        parts, order = [[]], []
        for action in program:
            parts[-1].append(action)
            if action[0] == "C":
                order.append((int(action[-2]), int(action[-1])))
                parts.append([])
        segments.append(parts)
        units.append(order)
    steps = len(units[0])

    lane = lax.broadcasted_iota(jnp.int32, (2 * PAIR, SPAN), 1)
    chosen = (lane % 32 == me % experts) & (lane < 96)

    def multiply(step):
        kind, k = jnp.int32(0), jnp.int32(0)
        for i in range(steps):
            for role in (0, 1):
                hit = (step == i) & (middle if role else jnp.logical_not(middle))
                kind = jnp.where(hit, units[role][i][0], kind)
                k = jnp.where(hit, units[role][i][1], k)
        unit = 4 * kind + k
        slot = step % 2
        gates = jnp.where(chosen, left[:, width:].astype(jnp.float32), 0.0)
        gates = jnp.sum(gates, axis=1, keepdims=True)
        tile = 256

        @pl.loop(0, half // tile)
        def _(j):
            at = pl.multiple_of(j * tile, tile)
            gate = jnp.dot(left[:, :width], w1[:, pl.ds(at, tile)], preferred_element_type=jnp.float32)
            up = jnp.dot(left[:, :width], w1[:, pl.ds(half + at, tile)], preferred_element_type=jnp.float32)
            hid[:, pl.ds(at, tile)] = (gate / (1.0 + jnp.exp(-gate)) * up * gates).astype(jnp.bfloat16)

        back = pltpu.make_async_remote_copy(
            src_ref=ps.at[slot], dst_ref=pp.at[kind, real(k)], send_sem=ps_send.at[slot],
            recv_sem=pr.at[kind, real(k)], device_id=where["p"], device_id_type=MESH,
        )

        @pl.when(step >= 2)
        def _():
            back.wait_send()

        wide = width // 4 if width % 1024 == 0 else width

        @pl.loop(0, width // wide)
        def _(j):
            at = pl.multiple_of(j * wide, wide)
            part = jnp.dot(hid[...], w2[:, pl.ds(at, wide)], preferred_element_type=jnp.float32)
            part = part.astype(jnp.bfloat16)
            held[unit, :, pl.ds(at, wide)] = part[:PAIR]
            ps[slot, :, pl.ds(at, wide)] = part[PAIR:]

        back.start()

    seen = [set(), set()]

    @pl.loop(0, steps)
    def _(step):
        for i in range(steps):
            for role in (0, 1):
                @pl.when((step == i) & (middle if role else jnp.logical_not(middle)))
                def _():
                    for action in segments[role][i]:
                        act(role, action, seen[role])

        @pl.when(step == 0)
        def _():
            for copy in weight_copies:
                copy.wait()

        multiply(step)

    for role in (0, 1):
        @pl.when(middle if role else jnp.logical_not(middle))
        def _():
            for action in segments[role][steps]:
                act(role, action, seen[role])
            for action in ORDER[role]:
                p, k = action[-2], int(action[-1])
                if action[0] == "S":
                    dispatch(role, action[1], p, k).wait_send()
                elif action[0] == "R":
                    if outgoing(role, p, k) == "f":
                        give(role, p, k).wait()
                    else:
                        give(role, p, k).wait_send()
    for slot in (0, 1):
        pltpu.make_async_remote_copy(
            src_ref=ps.at[slot], dst_ref=pp.at[0, 0], send_sem=ps_send.at[slot], recv_sem=pr.at[0, 0],
            device_id=where["p"], device_id_type=MESH,
        ).wait_send()


def fused(tokens, expert_ids, gate_weights, slot_expert, w_gate_up, w_down):
    devices = lax.axis_size("expert")
    experts = devices // 2
    rows, width = tokens.shape
    half = w_down.shape[1]
    chosen = expert_ids[:, :, None] == slot_expert[None, None, :experts]
    weights = jnp.sum(jnp.where(chosen, gate_weights[:, :, None], 0.0), axis=1)
    high = lax.reduce_precision(weights, 8, 7)
    mid = lax.reduce_precision(weights - high, 8, 7)
    low = weights - high - mid
    pad = jnp.zeros((rows, 32 - experts), jnp.float32)
    tail = jnp.concatenate([high, pad, mid, pad, low, pad, jnp.zeros((rows, 32), jnp.float32)], axis=1)
    wide = jnp.concatenate([tokens, tail.astype(jnp.bfloat16)], axis=1)
    full = width + SPAN
    bf16 = jnp.bfloat16
    rest = SPAN - HEAD
    shapes = [
        (rows, width),
        (2, 2, 4, rows, full),
        (3, 4, PAIR, width),
        (4, HEAD, width),
        (rest, width),
        (2, 4, HEAD, width),
        (2, 2, 4, rest, width),
    ]
    dma = pltpu.SemaphoreType.DMA
    results = pl.pallas_call(
        fused_kernel,
        out_shape=[jax.ShapeDtypeStruct(s, bf16) for s in shapes],
        in_specs=[pl.BlockSpec(memory_space=pl.ANY)] * 3,
        out_specs=[pl.BlockSpec(memory_space=pl.ANY)] * len(shapes),
        scratch_shapes=[
            pltpu.VMEM((width, 2 * half), bf16),
            pltpu.VMEM((half, width), bf16),
            pltpu.VMEM((2 * PAIR, full), bf16),
            pltpu.VMEM((2 * PAIR, half), bf16),
            pltpu.VMEM((12, PAIR, width), bf16),
            pltpu.VMEM((2, PAIR, width), bf16),
            pltpu.VMEM((4, FIRST, width), bf16),
            dma((2,)), dma((4,)), dma((4,)), dma((3,)),
            dma((4, 24)), dma((2, 24)), dma((2,)), dma((3, 4)), dma((24,)), dma((9,)), dma((2, 24)),
        ],
        compiler_params=pltpu.CompilerParams(
            collective_id=0, has_side_effects=True, vmem_limit_bytes=62 * 1024 * 1024
        ),
    )(wide, w_gate_up, w_down)
    return results[0]


def solution(mesh):
    return jax.shard_map(
        fused if mesh.shape["expert"] == 16 else per_device,
        mesh=mesh,
        in_specs=(
            P(("group", "expert"), None),
            P(("group", "expert"), None),
            P(("group", "expert"), None),
            P(),
            P("expert", None, None),
            P("expert", None, None),
        ),
        out_specs=P(("group", "expert"), None),
        check_vma=False,
    )
```
